128 devices in a mesh: fsdp: 8 (over z, core), ep: 16 (over x, y).
Axes of the slice: x: 4, y: 4, z: 4, core: 2. Of those that a mesh axis runs over, the one named last changes fastest.
Arguments:
- deltas: bfloat16 [16, 7168, 2048], P('ep', 'fsdp')
- sketch_matrix: bfloat16 [2048, 256], replicated, may hold values from -0.125 to 0.125
- owner_of: int32 [16], replicated, may hold values from 0 to 15, as said below
- serving: bfloat16 [32, 7168, 2048], P('ep', 'fsdp'), may hold values from -4 to 4
Outputs:
- updated: bfloat16 [32, 7168, 2048], P('ep', 'fsdp')
The draws below stay inside these ranges and needn't reach their ends.
Inputs may be any that keep to these rules, and one draw needn't show every extreme that they name: `owner_of`: each of the 16 owners owns at most 2 experts; in every draw some owner owns exactly 2 and some own none.
All inputs are finite; a program needn't handle non-finite values.
Results may differ from the reference program's by a relative error of at most 0.007.
Values may be sent and summed in bfloat16 or wider, within the bound.
No kernel may reach another device: no remote copies, remote signals or barrier semaphores. Data moves between devices by JAX's collectives and lax.ppermute only.
A program may use at most 128 MiB of HBM per device.

```python
import jax
import jax.numpy as jnp
from jax import lax

D = 7168
FF = 2048
RANK = 256
POWER = 2
SLOTS = 2
EXPERTS = 16
N_EP = 16


def draw_deltas(key, part):
    base = jax.random.fold_in(key, 23)
    values = jnp.clip(jax.random.normal(base, (EXPERTS, D, FF), jnp.float32), -6.0, 6.0)
    return values.astype(jnp.bfloat16)


def draw_owner_of(key, part):
    base = jax.random.fold_in(key, 11)
    key_pairs, key_owners, key_order, key_experts = jax.random.split(base, 4)
    total = EXPERTS
    paired = jax.random.randint(key_pairs, (), 1, total // 2 + 1)
    position = jnp.arange(total, dtype=jnp.int32)
    middle = (1 + jax.random.permutation(key_owners, total - 2)).astype(jnp.int32)
    candidates = jnp.concatenate([jnp.array([0, total - 1], jnp.int32), middle])
    scores = jax.random.permutation(key_order, total).astype(jnp.int32)
    scores = scores + jnp.where(position < total - paired, 0, total).astype(jnp.int32)
    order = jnp.argsort(scores, stable=True)
    owner_perm = candidates[order]
    source = jnp.where(position < 2 * paired, position // 2, position - paired)
    assigned = owner_perm[source].astype(jnp.int32)
    expert_perm = jax.random.permutation(key_experts, total)
    return jnp.zeros((total,), jnp.int32).at[expert_perm].set(assigned)


def block_levels(own_key, extent, pieces, least, top_value):
    loudness, own = 1.0, jax.random.fold_in(own_key, 6)
    for dim, shards_of in pieces:
        steps = jnp.exp(jax.random.uniform(jax.random.fold_in(own, dim), (shards_of,), jnp.float32, least / len(pieces), top_value / len(pieces)))
        loudness = loudness * jnp.repeat(steps, extent[dim] // shards_of).reshape([-1 if axis == dim else 1 for axis in range(len(extent))])
    return loudness


def scatter_about(rng, shape, width, reach, cuts=(), kind=jnp.bfloat16):
    drawn = jax.random.normal(rng, shape, jnp.float32) * width
    if len(cuts) > 0:
        drawn = block_levels(rng, shape, cuts, -0.22, 0.18) * drawn
    return jnp.clip(drawn, min=-reach, max=reach).astype(kind)


def setup_inputs(seed: int = 0) -> dict:
    keys = jax.random.split(jax.random.key(seed), 5)
    return {
        "deltas": draw_deltas(jax.random.fold_in(keys[4], 71), 0),
        "sketch_matrix": scatter_about(keys[1], (FF, RANK), FF ** -0.5, 0.125),
        "owner_of": draw_owner_of(jax.random.fold_in(keys[4], 71), 0),
        "serving": scatter_about(keys[3], (N_EP * SLOTS, D, FF), 0.5, 4.0, ((0, 16), (1, 8))),
    }


def sketch_one(delta_one, sketch_matrix):
    contract = (((0,), (0,)), ((), ()))
    current = jnp.dot(delta_one.astype(jnp.float32), sketch_matrix.astype(jnp.float32), preferred_element_type=jnp.float32).astype(jnp.bfloat16)
    for iteration in range(POWER):
        power_step = lax.dot_general(delta_one.astype(jnp.float32), current.astype(jnp.float32), contract, preferred_element_type=jnp.float32)
        power_step = (power_step / D).astype(jnp.bfloat16)
        current = jnp.dot(delta_one.astype(jnp.float32), power_step.astype(jnp.float32), preferred_element_type=jnp.float32).astype(jnp.bfloat16)
    gram_total = lax.dot_general(current.astype(jnp.float32), current.astype(jnp.float32), contract, preferred_element_type=jnp.float32)
    cross_total = lax.dot_general(current.astype(jnp.float32), delta_one.astype(jnp.float32), contract, preferred_element_type=jnp.float32)
    factor_low = jnp.linalg.cholesky(gram_total)
    basis_rows = lax.linalg.triangular_solve(factor_low, current.astype(jnp.float32).T, left_side=True, lower=True)
    coeffs = lax.linalg.triangular_solve(factor_low, cross_total, left_side=True, lower=True)
    return (basis_rows.astype(jnp.bfloat16), coeffs.astype(jnp.bfloat16))

def reference(deltas, sketch_matrix, owner_of, serving):
    basis_all, coeff_all = lax.map(lambda delta_one: sketch_one(delta_one, sketch_matrix), deltas)
    expert_ids = jnp.arange(EXPERTS, dtype=jnp.int32)

    def rebuild(slot_index):
        owner_now = slot_index // SLOTS
        place_now = slot_index % SLOTS
        is_owned = (owner_of == owner_now).astype(jnp.int32)
        owned_rank = jnp.cumsum(is_owned, dtype=jnp.int32) - 1
        slot_hits = (is_owned == 1) & (owned_rank == place_now)
        present = jnp.any(slot_hits)
        chosen = jnp.sum(jnp.where(slot_hits, expert_ids, 0)).astype(jnp.int32)
        update = lax.dot_general(basis_all[chosen].astype(jnp.float32), coeff_all[chosen].astype(jnp.float32), (((0,), (0,)), ((), ())), preferred_element_type=jnp.float32)
        summed = serving[slot_index].astype(jnp.float32) + jnp.where(present, update, jnp.float32(0.0))
        return summed.astype(jnp.bfloat16)
    return lax.map(rebuild, jnp.arange(N_EP * SLOTS, dtype=jnp.int32))
```

```python
import jax
import jax.numpy as jnp
from jax import lax
from jax.experimental import pallas as pl
from jax.experimental.pallas import tpu as pltpu
from jax.sharding import Mesh, PartitionSpec as P

D = 7168
FF = 2048
RANK = 256
POWER = 2
SLOTS = 2
N_EP = 16
EP = ("x", "y")
SWAP = [(0, 1), (1, 0)]
CONTRACT = (((0,), (0,)), ((), ()))
NT = (((1,), (1,)), ((), ()))
F32 = jnp.float32
BF16 = jnp.bfloat16


def halves(part, c):
    pair = part.reshape((2, part.shape[0] // 2) + part.shape[1:])
    mine = lax.dynamic_index_in_dim(pair, c, 0, keepdims=False)
    other = lax.dynamic_index_in_dim(pair, 1 - c, 0, keepdims=False)
    return mine, other


def join(mine, other, c, axis=0):
    return jnp.where(
        c == 0,
        jnp.concatenate([mine, other], axis=axis),
        jnp.concatenate([other, mine], axis=axis),
    )


def chip_sum(part, c):
    mine, other = halves(part, c)
    received = lax.ppermute(other.astype(BF16), "c", SWAP)
    return (mine + received.astype(F32)).astype(BF16)


def all_sum(part, c):
    summed = chip_sum(part, c).reshape(4, FF // 8, RANK)
    pieces = lax.all_to_all(summed, "z", 0, 0, tiled=True)
    step = (jnp.sum(pieces.astype(F32), axis=0) / D).astype(BF16)
    mine = lax.all_gather(step, "z", axis=0, tiled=True)
    other = lax.ppermute(mine, "c", SWAP)
    return join(mine, other, c)


def final_kernel(sel_ref, present_ref, y_ref, m_ref, serving_ref, out_ref):
    slot = pl.program_id(0)
    update = lax.dot_general(y_ref[0], m_ref[0], NT, preferred_element_type=F32)
    served = serving_ref[0].astype(F32)
    summed = served + jnp.where(present_ref[slot] > 0, update, 0.0)
    out_ref[0] = summed.astype(BF16)


def final(sel, present, y_all, m_sel, serving):
    slots, rows, cols = serving.shape
    tile = 448
    spec = pltpu.PrefetchScalarGridSpec(
        num_scalar_prefetch=2,
        grid=(slots, rows // tile),
        in_specs=[
            pl.BlockSpec((1, tile, RANK), lambda s, r, sel, pr: (sel[s], r, 0)),
            pl.BlockSpec((1, cols, RANK), lambda s, r, sel, pr: (s, 0, 0)),
            pl.BlockSpec((1, tile, cols), lambda s, r, sel, pr: (s, r, 0)),
        ],
        out_specs=pl.BlockSpec((1, tile, cols), lambda s, r, sel, pr: (s, r, 0)),
    )
    return pl.pallas_call(
        final_kernel,
        grid_spec=spec,
        out_shape=jax.ShapeDtypeStruct(serving.shape, BF16),
        compiler_params=pltpu.CompilerParams(
            dimension_semantics=("arbitrary", "arbitrary"), vmem_limit_bytes=40 << 20
        ),
        name="final",
    )(sel, present, y_all, m_sel, serving)


def local(deltas, sketch_matrix, owner_of, serving):
    c = lax.axis_index("c")
    own_index = lax.axis_index("x") * 4 + lax.axis_index("y")
    delta_rows = deltas[0]
    current = jnp.dot(delta_rows, sketch_matrix, preferred_element_type=F32).astype(BF16)
    for iteration in range(POWER):
        part = lax.dot_general(delta_rows, current, CONTRACT, preferred_element_type=F32)
        power_step = all_sum(part, c)
        current = jnp.dot(delta_rows, power_step, preferred_element_type=F32).astype(BF16)

    y_all = lax.all_gather(current, EP, axis=0).reshape(N_EP, -1, RANK)

    cross_part = lax.dot_general(delta_rows, current, CONTRACT, preferred_element_type=F32)
    gram_part = lax.dot_general(current, current, CONTRACT, preferred_element_type=F32)
    gram_mine, gram_other = halves(gram_part, c)
    gram_chip = gram_mine + lax.ppermute(gram_other, "c", SWAP)
    gram_hi = lax.reduce_precision(gram_chip, 8, 7)
    gram_lo = (gram_chip - gram_hi).astype(BF16)
    gram_pair = jnp.concatenate([gram_hi.astype(BF16), gram_lo], axis=0)
    cross_chip = chip_sum(cross_part, c).reshape(4, FF // 8, RANK)
    packed = jnp.concatenate(
        [cross_chip, jnp.broadcast_to(gram_pair[None], (4, RANK, RANK))], axis=1
    )
    pieces = lax.all_to_all(packed, "z", 0, 0, tiled=True)
    sums = jnp.sum(pieces.astype(F32), axis=0)
    cross = sums[: FF // 8]
    gram_half = sums[FF // 8 : FF // 8 + RANK // 2] + sums[FF // 8 + RANK // 2 :]
    gram = join(gram_half, lax.ppermute(gram_half, "c", SWAP), c)

    factor_low = jnp.linalg.cholesky(gram)
    solved = lax.linalg.triangular_solve(
        factor_low, cross, left_side=False, lower=True, transpose_a=True
    )
    solved = lax.linalg.triangular_solve(
        factor_low, solved, left_side=False, lower=True, transpose_a=False
    ).astype(BF16)

    is_owned = (owner_of == own_index).astype(jnp.int32)
    owned_rank = jnp.cumsum(is_owned, dtype=jnp.int32) - 1
    slot_ids = jnp.arange(SLOTS, dtype=jnp.int32)
    slot_hits = (is_owned[None, :] == 1) & (owned_rank[None, :] == slot_ids[:, None])
    present = jnp.any(slot_hits, axis=1).astype(jnp.int32)
    expert_ids = jnp.arange(N_EP, dtype=jnp.int32)
    sel = jnp.sum(jnp.where(slot_hits, expert_ids[None, :], 0), axis=1).astype(jnp.int32)

    chunks = lax.all_to_all(
        jnp.broadcast_to(solved[None], (N_EP,) + solved.shape), EP, 0, 0, tiled=True
    )
    picked = jnp.stack(
        [lax.dynamic_index_in_dim(chunks, sel[s], 0, keepdims=False) for s in range(SLOTS)]
    )
    halves_z = lax.all_to_all(
        jnp.broadcast_to(picked[None], (4,) + picked.shape), "z", 0, 0, tiled=True
    )
    m_mine = halves_z.transpose(1, 0, 2, 3).reshape(SLOTS, FF // 2, RANK)
    m_other = lax.ppermute(m_mine, "c", SWAP)
    m_sel = join(m_mine, m_other, c, axis=1)
    return final(sel, present, y_all, m_sel, serving)


def solution(mesh):
    split = Mesh(mesh.devices.reshape(4, 2, 4, 4), ("z", "c", "x", "y"))
    rows = P(EP, ("z", "c"), None)
    return jax.shard_map(
        local,
        mesh=split,
        in_specs=(rows, P(), P(), rows),
        out_specs=rows,
        check_vma=False,
    )
```

```python
import jax
import jax.numpy as jnp
from jax import lax
from jax.experimental import pallas as pl
from jax.experimental.pallas import tpu as pltpu
from jax.sharding import Mesh, PartitionSpec as P

D = 7168
FF = 2048
RANK = 256
POWER = 2
SLOTS = 2
N_EP = 16
HALF = RANK // 2
GROUP = 8
CHUNK = FF // 8
SPANS = ((0, 256), (256, 256), (512, 384))
EP = ("x", "y")
SWAP = [(0, 1), (1, 0)]
NT = (((1,), (1,)), ((), ()))
F32 = jnp.float32
BF16 = jnp.bfloat16
VM = pl.BlockSpec(memory_space=pltpu.VMEM)
SM = pl.BlockSpec(memory_space=pltpu.SMEM)
ANY = pl.BlockSpec(memory_space=pl.ANY)


def columns(half, j):
    return pl.ds(pl.multiple_of(half * (FF // 2) + j * CHUNK, CHUNK), CHUNK)


def load_rows(a_hbm, a_ref, sems):
    copies = [
        pltpu.make_async_copy(a_hbm.at[pl.ds(s, n)], a_ref.at[pl.ds(s, n)], sems.at[i])
        for i, (s, n) in enumerate(SPANS)
    ]
    for copy in copies:
        copy.start()
    return copies


def power_tiles(c, a_ref, yt_ref, mine_out, other_out):
    for j in range(4):
        tile = jnp.dot(yt_ref[...], a_ref[:, columns(1 - c, j)], preferred_element_type=F32)
        other_out[j] = tile.astype(BF16)
    for j in range(4):
        mine_out[j] = jnp.dot(
            yt_ref[...], a_ref[:, columns(c, j)], preferred_element_type=F32
        )


def sketch_rows(c, a_ref, s, n, mine_ref, other_ref):
    y = None
    for half, steps in ((c, mine_ref), (1 - c, other_ref)):
        for j in range(4):
            term = lax.dot_general(
                a_ref[pl.ds(s, n), columns(half, j)], steps[j], NT, preferred_element_type=F32
            )
            y = term if y is None else y + term
    return y


def first_kernel(c_ref, a_hbm, sketch_ref, mine_out, other_out, a_ref, yt_ref, sems):
    c = c_ref[0]
    copies = load_rows(a_hbm, a_ref, sems)
    for copy, (s, n) in zip(copies, SPANS):
        copy.wait()
        y = jnp.dot(a_ref[pl.ds(s, n), :], sketch_ref[...], preferred_element_type=F32)
        yt_ref[:, pl.ds(s, n)] = y.T.astype(BF16)
    power_tiles(c, a_ref, yt_ref, mine_out, other_out)


def power_kernel(c_ref, a_hbm, mine_ref, other_ref, mine_out, other_out, a_ref, yt_ref, sems):
    c = c_ref[0]
    copies = load_rows(a_hbm, a_ref, sems)
    for copy, (s, n) in zip(copies, SPANS):
        copy.wait()
        y = sketch_rows(c, a_ref, s, n, mine_ref, other_ref)
        yt_ref[:, pl.ds(s, n)] = y.T.astype(BF16)
    power_tiles(c, a_ref, yt_ref, mine_out, other_out)


def last_kernel(
    c_ref, a_hbm, mine_ref, other_ref,
    y_out, mine_out, other_out, gram_mine, gram_other, a_ref, yt_ref, sems,
):
    c = c_ref[0]
    copies = load_rows(a_hbm, a_ref, sems)
    for copy, (s, n) in zip(copies, SPANS):
        copy.wait()
        y = sketch_rows(c, a_ref, s, n, mine_ref, other_ref)
        y_out[pl.ds(s, n), :] = y.astype(BF16)
        yt_ref[:, pl.ds(s, n)] = y.T.astype(BF16)
    for half, out in ((1 - c, gram_other), (c, gram_mine)):
        turned = yt_ref[pl.ds(pl.multiple_of(half * HALF, HALF), HALF), :]
        out[...] = jnp.dot(turned, y_out[...], preferred_element_type=F32)
    power_tiles(c, a_ref, yt_ref, mine_out, other_out)


def sweep(kernel, operands, extra, name):
    rows = operands[1].shape[0]
    tiles = (4, RANK, CHUNK)
    outs = extra[:1] + [
        jax.ShapeDtypeStruct(tiles, F32), jax.ShapeDtypeStruct(tiles, BF16)
    ] + extra[1:]
    return pl.pallas_call(
        kernel,
        in_specs=[SM, ANY] + [VM] * (len(operands) - 2),
        out_specs=[VM] * len(outs),
        out_shape=outs,
        scratch_shapes=[
            pltpu.VMEM((rows, FF), BF16),
            pltpu.VMEM((RANK, rows), BF16),
            pltpu.SemaphoreType.DMA((len(SPANS),)),
        ],
        compiler_params=pltpu.CompilerParams(vmem_limit_bytes=24 << 20),
        name=name,
    )(*operands)


def exact_dot(a, b):
    return jnp.dot(a, b, preferred_element_type=F32, precision=lax.Precision.HIGHEST)


def invert(a_ref, cols_ref):
    lane = lax.broadcasted_iota(jnp.int32, (GROUP, HALF), 1)
    sub = lax.broadcasted_iota(jnp.int32, (GROUP, HALF), 0)
    lane_all = lax.broadcasted_iota(jnp.int32, (HALF, HALF), 1)

    def group(g, carry):
        base = pl.multiple_of(g * GROUP, GROUP)
        rows = a_ref[pl.ds(base, GROUP), :]
        turned = rows.T
        for i in range(GROUP):
            cols_ref[i] = jnp.broadcast_to(turned[:, i : i + 1], (HALF, HALF))
        block = [cols_ref[i, pl.ds(base, GROUP), :] for i in range(GROUP)]
        for j in range(GROUP):
            inverse = 1.0 / jnp.broadcast_to(block[j][j : j + 1], (GROUP, HALF))
            new = []
            for i in range(GROUP):
                if i == j:
                    new.append(jnp.where(sub == j, -inverse, block[j] * inverse))
                else:
                    t = jnp.broadcast_to(block[i][j : j + 1], (GROUP, HALF)) * inverse
                    new.append(jnp.where(sub == j, t, block[i] - block[j] * t))
            block = new
        local = lane - base
        rows = jnp.where((local >= 0) & (local < GROUP), jnp.where(local == sub, 1.0, 0.0), -rows)
        solved = block[0] * jnp.broadcast_to(rows[0:1], (GROUP, HALF))
        for i in range(1, GROUP):
            solved = solved + block[i] * jnp.broadcast_to(rows[i : i + 1], (GROUP, HALF))
        here = lane_all - base
        a = jnp.where((here >= 0) & (here < GROUP), 0.0, a_ref[...])
        for i in range(GROUP):
            a = a - cols_ref[i] * jnp.broadcast_to(solved[i : i + 1], (HALF, HALF))
        a_ref[...] = a
        a_ref[pl.ds(base, GROUP), :] = solved
        return carry

    lax.fori_loop(0, HALF // GROUP, group, 0)


def solve_kernel(c_ref, mine_ref, other_ref, cross_ref, out_ref, a_ref, b_ref, cols_ref, gram_ref):
    c = c_ref[0]
    gram_ref[pl.ds(pl.multiple_of(c * HALF, HALF), HALF), :] = mine_ref[...]
    gram_ref[pl.ds(pl.multiple_of((1 - c) * HALF, HALF), HALF), :] = other_ref[...]
    a_ref[...] = gram_ref[:HALF, :HALF]
    invert(a_ref, cols_ref)
    first = -a_ref[...]
    across = gram_ref[:HALF, HALF:]
    step = exact_dot(first, across)
    b_ref[...] = gram_ref[HALF:, HALF:] - exact_dot(across.T, step)
    invert(b_ref, cols_ref)
    top = cross_ref[:HALF]
    low = cross_ref[HALF:]
    low_solved = -exact_dot(b_ref[...], low - exact_dot(step.T, top))
    top_solved = exact_dot(first, top) - exact_dot(step, low_solved)
    top_solved = top_solved.astype(BF16)
    low_solved = low_solved.astype(BF16)
    for e in range(N_EP):
        out_ref[e, :HALF] = top_solved
        out_ref[e, HALF:] = low_solved


def solve(c, gram_mine, gram_other, cross):
    vm = pl.BlockSpec(memory_space=pltpu.VMEM)
    return pl.pallas_call(
        solve_kernel,
        in_specs=[pl.BlockSpec(memory_space=pltpu.SMEM), vm, vm, vm],
        out_specs=vm,
        out_shape=jax.ShapeDtypeStruct((N_EP, RANK, cross.shape[1]), BF16),
        scratch_shapes=[
            pltpu.VMEM((HALF, HALF), F32),
            pltpu.VMEM((HALF, HALF), F32),
            pltpu.VMEM((GROUP, HALF, HALF), F32),
            pltpu.VMEM((RANK, RANK), F32),
        ],
        compiler_params=pltpu.CompilerParams(vmem_limit_bytes=12 << 20),
        name="solve",
    )(c, gram_mine, gram_other, cross)


def chip_sum(mine, other):
    return mine + lax.ppermute(other, "c", SWAP).astype(F32)


def all_sum(mine, other):
    chip = chip_sum(mine, other).astype(BF16)
    pieces = lax.all_to_all(chip, "z", 0, 0, tiled=True)
    step = (jnp.sum(pieces.astype(F32), axis=0) / D).astype(BF16)
    step_mine = lax.all_gather(step, "z", axis=0)
    return step_mine, lax.ppermute(step_mine, "c", SWAP)


def final_kernel(sel_ref, present_ref, c_ref, y_ref, mine_ref, other_ref, serving_ref, out_ref):
    slot = pl.program_id(0)
    c = c_ref[0]
    owned = present_ref[slot] > 0
    for half, solved in ((c, mine_ref), (1 - c, other_ref)):
        for j in range(4):
            update = jnp.dot(y_ref[0], solved[j, 0], preferred_element_type=F32)
            served = serving_ref[0, :, columns(half, j)].astype(F32)
            summed = served + jnp.where(owned, update, 0.0)
            out_ref[0, :, columns(half, j)] = summed.astype(BF16)


def final(sel, present, c, y_all, mine, other, serving):
    slots, rows, cols = serving.shape
    tile = 448
    block = pl.BlockSpec((1, tile, cols), lambda s, r, sel, pr, c: (s, r, 0))
    chunks = pl.BlockSpec((4, 1, RANK, CHUNK), lambda s, r, sel, pr, c: (0, s, 0, 0))
    spec = pltpu.PrefetchScalarGridSpec(
        num_scalar_prefetch=3,
        grid=(slots, rows // tile),
        in_specs=[
            pl.BlockSpec((1, tile, RANK), lambda s, r, sel, pr, c: (sel[s], r, 0)),
            chunks,
            chunks,
            block,
        ],
        out_specs=block,
    )
    return pl.pallas_call(
        final_kernel,
        grid_spec=spec,
        out_shape=jax.ShapeDtypeStruct(serving.shape, BF16),
        compiler_params=pltpu.CompilerParams(
            dimension_semantics=("arbitrary", "arbitrary"), vmem_limit_bytes=32 << 20
        ),
        name="final",
    )(sel, present, c, y_all, mine, other, serving)


def local(deltas, sketch_matrix, owner_of, serving):
    c = lax.axis_index("c").astype(jnp.int32).reshape(1)
    own_index = lax.axis_index("x") * 4 + lax.axis_index("y")
    delta_rows = deltas[0]
    rows = delta_rows.shape[0]
    mine, other = sweep(first_kernel, [c, delta_rows, sketch_matrix], [], "first")
    for iteration in range(POWER - 1):
        step_mine, step_other = all_sum(mine, other)
        mine, other = sweep(power_kernel, [c, delta_rows, step_mine, step_other], [], "power")
    step_mine, step_other = all_sum(mine, other)
    extra = [jax.ShapeDtypeStruct((rows, RANK), BF16)] + [
        jax.ShapeDtypeStruct((HALF, RANK), F32)
    ] * 2
    sketch, mine, other, gram_mine, gram_other = sweep(
        last_kernel, [c, delta_rows, step_mine, step_other], extra, "last"
    )
    y_all = lax.all_gather(sketch, EP, axis=0)

    gram_chip = chip_sum(gram_mine, gram_other)
    gram_hi = lax.reduce_precision(gram_chip, 8, 7)
    gram_lo = (gram_chip - gram_hi).astype(BF16)
    gram_pair = jnp.concatenate([gram_hi.astype(BF16), gram_lo], axis=0)
    cross_chip = chip_sum(mine, other).astype(BF16)
    packed = jnp.concatenate(
        [cross_chip, jnp.broadcast_to(gram_pair[None], (4, RANK, RANK))], axis=1
    )
    pieces = lax.all_to_all(packed, "z", 0, 0, tiled=True)
    sums = jnp.sum(pieces.astype(F32), axis=0)
    cross = sums[:RANK]
    gram_half = sums[RANK : RANK + HALF] + sums[RANK + HALF :]
    solved = solve(c, gram_half, lax.ppermute(gram_half, "c", SWAP), cross)

    is_owned = (owner_of == own_index).astype(jnp.int32)
    owned_rank = jnp.cumsum(is_owned, dtype=jnp.int32) - 1
    slot_ids = jnp.arange(SLOTS, dtype=jnp.int32)
    slot_hits = (is_owned[None, :] == 1) & (owned_rank[None, :] == slot_ids[:, None])
    present = jnp.any(slot_hits, axis=1).astype(jnp.int32)
    expert_ids = jnp.arange(N_EP, dtype=jnp.int32)
    sel = jnp.sum(jnp.where(slot_hits, expert_ids[None, :], 0), axis=1).astype(jnp.int32)

    chunks = lax.all_to_all(solved, EP, 0, 0, tiled=True)
    picked = jnp.stack(
        [lax.dynamic_index_in_dim(chunks, sel[s], 0, keepdims=False) for s in range(SLOTS)]
    )
    solved_mine = lax.all_to_all(
        jnp.broadcast_to(picked[None], (4,) + picked.shape), "z", 0, 0, tiled=True
    )
    solved_other = lax.ppermute(solved_mine, "c", SWAP)
    return final(sel, present, c, y_all, solved_mine, solved_other, serving)


def solution(mesh):
    split = Mesh(mesh.devices.reshape(4, 2, 4, 4), ("z", "c", "x", "y"))
    rows = P(EP, ("z", "c"), None)
    return jax.shard_map(
        local,
        mesh=split,
        in_specs=(rows, P(), P(), rows),
        out_specs=rows,
        check_vma=False,
    )
```

```python
import jax
import jax.numpy as jnp
from jax import lax
from jax.experimental import pallas as pl
from jax.experimental.pallas import tpu as pltpu
from jax.sharding import Mesh, PartitionSpec as P

D = 7168
FF = 2048
RANK = 256
POWER = 2
SLOTS = 2
N_EP = 16
HALF = RANK // 2
GROUP = 16
CHUNK = FF // 8
SPANS = ((0, 256), (256, 256), (512, 384))
EP = ("x", "y")
SEND, FROM, EXPERT, PRESENT = 0, 8, 10, 12
TILE = 224
SWAP = [(0, 1), (1, 0)]
NT = (((1,), (1,)), ((), ()))
F32 = jnp.float32
BF16 = jnp.bfloat16
VM = pl.BlockSpec(memory_space=pltpu.VMEM)
SM = pl.BlockSpec(memory_space=pltpu.SMEM)
HBM = pl.BlockSpec(memory_space=pltpu.HBM)
TILES = (4, RANK, CHUNK)


def columns(half, j):
    return pl.ds(pl.multiple_of(half * (FF // 2) + j * CHUNK, CHUNK), CHUNK)


def load_rows(a_hbm, a_ref, sems):
    copies = [
        pltpu.make_async_copy(a_hbm.at[pl.ds(s, n)], a_ref.at[pl.ds(s, n)], sems.at[i])
        for i, (s, n) in enumerate(SPANS)
    ]
    for copy in copies:
        copy.start()
    return copies


def power_tiles(c, a_ref, yt_ref, mine_out, other_out):
    for j in range(4):
        tile = jnp.dot(yt_ref[...], a_ref[:, columns(1 - c, j)], preferred_element_type=F32)
        other_out[j] = tile.astype(BF16)
    for j in range(4):
        mine_out[j] = jnp.dot(
            yt_ref[...], a_ref[:, columns(c, j)], preferred_element_type=F32
        )


def sketch_rows(c, a_ref, s, n, mine_ref, other_ref):
    y = None
    for half, steps in ((c, mine_ref), (1 - c, other_ref)):
        for j in range(4):
            term = lax.dot_general(
                a_ref[pl.ds(s, n), columns(half, j)], steps[j], NT, preferred_element_type=F32
            )
            y = term if y is None else y + term
    return y


def first_kernel(
    c_ref, a_hbm, sketch_hbm, mine_out, other_out, a_ref, sketch_ref, yt_ref, sems, sketch_sem
):
    c = c_ref[0]
    sketch_copy = pltpu.make_async_copy(sketch_hbm, sketch_ref, sketch_sem)
    sketch_copy.start()
    copies = load_rows(a_hbm, a_ref, sems)
    sketch_copy.wait()
    for copy, (s, n) in zip(copies, SPANS):
        copy.wait()
        y = jnp.dot(a_ref[pl.ds(s, n), :], sketch_ref[...], preferred_element_type=F32)
        yt_ref[:, pl.ds(s, n)] = y.T.astype(BF16)
    power_tiles(c, a_ref, yt_ref, mine_out, other_out)


def power_kernel(c_ref, a_ref, mine_ref, other_ref, mine_out, other_out, yt_ref):
    c = c_ref[0]
    for s, n in SPANS:
        y = sketch_rows(c, a_ref, s, n, mine_ref, other_ref)
        yt_ref[:, pl.ds(s, n)] = y.T.astype(BF16)
    power_tiles(c, a_ref, yt_ref, mine_out, other_out)


def last_kernel(
    c_ref, a_ref, mine_ref, other_ref,
    y_out, mine_out, other_out, gram_mine, gram_other, yt_ref,
):
    c = c_ref[0]
    for s, n in SPANS:
        y = sketch_rows(c, a_ref, s, n, mine_ref, other_ref)
        y_out[pl.ds(s, n), :] = y.astype(BF16)
        yt_ref[:, pl.ds(s, n)] = y.T.astype(BF16)
    for half, out in ((1 - c, gram_other), (c, gram_mine)):
        turned = yt_ref[pl.ds(pl.multiple_of(half * HALF, HALF), HALF), :]
        out[...] = jnp.dot(turned, y_out[...], preferred_element_type=F32)
    power_tiles(c, a_ref, yt_ref, mine_out, other_out)


def first_pass(c, delta_rows, sketch_matrix):
    rows = delta_rows.shape[0]
    return pl.pallas_call(
        first_kernel,
        in_specs=[SM, HBM, HBM],
        out_specs=[VM] * 2,
        out_shape=[
            jax.ShapeDtypeStruct(TILES, F32),
            jax.ShapeDtypeStruct(TILES, BF16),
        ],
        scratch_shapes=[
            pltpu.VMEM(delta_rows.shape, BF16),
            pltpu.VMEM(sketch_matrix.shape, BF16),
            pltpu.VMEM((RANK, rows), BF16),
            pltpu.SemaphoreType.DMA((len(SPANS),)),
            pltpu.SemaphoreType.DMA,
        ],
        compiler_params=pltpu.CompilerParams(vmem_limit_bytes=16 << 20),
        name="first",
    )(
        c,
        pltpu.with_memory_space_constraint(delta_rows, pltpu.HBM),
        pltpu.with_memory_space_constraint(sketch_matrix, pltpu.HBM),
    )


def power_pass(kernel, c, delta_rows, steps, before, after, name):
    outs = before + [
        jax.ShapeDtypeStruct(TILES, F32), jax.ShapeDtypeStruct(TILES, BF16)
    ] + after
    return pl.pallas_call(
        kernel,
        in_specs=[SM, VM, VM, VM],
        out_specs=[VM] * len(outs),
        out_shape=outs,
        scratch_shapes=[pltpu.VMEM((RANK, delta_rows.shape[0]), BF16)],
        compiler_params=pltpu.CompilerParams(vmem_limit_bytes=24 << 20),
        name=name,
    )(c, delta_rows, *steps)


def exact_dot(a, b):
    return jnp.dot(a, b, preferred_element_type=F32, precision=lax.Precision.HIGHEST)


def invert(a_ref):
    lane = lax.broadcasted_iota(jnp.int32, (GROUP, HALF), 1)
    sub = lax.broadcasted_iota(jnp.int32, (GROUP, HALF), 0)
    lane_all = lax.broadcasted_iota(jnp.int32, (HALF, HALF), 1)

    def spread(row):
        return jnp.broadcast_to(row, (GROUP, HALF))

    def columns_of(rows, base):
        return [jnp.broadcast_to(rows[:, base + i : base + i + 1], (GROUP, HALF)) for i in range(GROUP)]

    def total(terms):
        while len(terms) > 1:
            terms = [terms[i] + terms[i + 1] for i in range(0, len(terms), 2)]
        return terms[0]

    def pivots(base, rows):
        block = columns_of(rows, base)
        for j in range(GROUP):
            inverse = 1.0 / spread(block[j][j : j + 1])
            scaled = block[j] * inverse
            new = []
            for i in range(GROUP):
                if i == j:
                    new.append(jnp.where(sub == j, -inverse, scaled))
                else:
                    t = spread(block[i][j : j + 1])
                    new.append(jnp.where(sub == j, t * inverse, block[i] - scaled * t))
            block = new
        local = lane - base
        rows = jnp.where((local >= 0) & (local < GROUP), jnp.where(local == sub, 1.0, 0.0), -rows)
        return total([block[i] * spread(rows[i : i + 1]) for i in range(GROUP)])

    rows = a_ref[:GROUP, :]
    solved = pivots(0, rows)
    for base in range(0, HALF, GROUP):
        later = base + GROUP
        if later < HALF:
            local = lane - base
            ahead = a_ref[later : later + GROUP, :]
            across = columns_of(ahead, base)
            ahead = jnp.where((local >= 0) & (local < GROUP), 0.0, ahead)
            ahead = ahead - total([across[i] * spread(solved[i : i + 1]) for i in range(GROUP)])
            ahead_solved = pivots(later, ahead)
        here = lane_all - base
        a = jnp.where((here >= 0) & (here < GROUP), 0.0, a_ref[...])
        a_ref[...] = a - lax.dot_general(
            rows, solved, (((0,), (0,)), ((), ())),
            preferred_element_type=F32, precision=lax.Precision.HIGHEST,
        )
        a_ref[base : base + GROUP, :] = solved
        if later < HALF:
            rows, solved = ahead, ahead_solved


def slots_of(owner_ref, owner):
    zero = jnp.int32(0)
    count, expert = zero, [zero] * SLOTS
    for e in range(N_EP):
        hit = owner_ref[e] == owner
        for s in range(SLOTS):
            expert[s] = jnp.where(hit & (count == s), e, expert[s])
        count = count + jnp.where(hit, 1, 0)
    return expert, [jnp.where(count > s, 1, 0) for s in range(SLOTS)]


def write_table(place_ref, owner_ref, table_ref):
    x, y = place_ref[1], place_ref[2]
    for there in range(4):
        expert, _ = slots_of(owner_ref, x * 4 + there)
        for s in range(SLOTS):
            table_ref[SEND + there * SLOTS + s] = expert[s] // 4
    expert, present = slots_of(owner_ref, x * 4 + y)
    for s in range(SLOTS):
        table_ref[FROM + s] = lax.rem(expert[s], 4)
        table_ref[EXPERT + s] = expert[s]
        table_ref[PRESENT + s] = present[s]


def solve_kernel(
    place_ref, owner_ref, mine_ref, other_ref, cross_ref, out_ref, table_ref, a_ref, b_ref, gram_ref
):
    write_table(place_ref, owner_ref, table_ref)
    c = place_ref[0]
    gram_ref[pl.ds(pl.multiple_of(c * HALF, HALF), HALF), :] = mine_ref[...]
    gram_ref[pl.ds(pl.multiple_of((1 - c) * HALF, HALF), HALF), :] = other_ref[...]
    a_ref[...] = gram_ref[:HALF, :HALF]
    invert(a_ref)
    first = -a_ref[...]
    across = gram_ref[:HALF, HALF:]
    step = exact_dot(first, across)
    b_ref[...] = gram_ref[HALF:, HALF:] - exact_dot(across.T, step)
    invert(b_ref)
    top = cross_ref[:HALF]
    low = cross_ref[HALF:]
    low_solved = -exact_dot(b_ref[...], low - exact_dot(step.T, top))
    top_solved = exact_dot(first, top) - exact_dot(step, low_solved)
    top_solved = top_solved.astype(BF16)
    low_solved = low_solved.astype(BF16)
    for x in range(4):
        out_ref[x, :HALF] = top_solved
        out_ref[x, HALF:] = low_solved


def solve(place, owner_of, gram_mine, gram_other, cross):
    return pl.pallas_call(
        solve_kernel,
        in_specs=[SM, SM, VM, VM, VM],
        out_specs=[VM, SM],
        out_shape=[
            jax.ShapeDtypeStruct((4, RANK, cross.shape[1]), BF16),
            jax.ShapeDtypeStruct((16,), jnp.int32),
        ],
        scratch_shapes=[
            pltpu.VMEM((HALF, HALF), F32),
            pltpu.VMEM((HALF, HALF), F32),
            pltpu.VMEM((RANK, RANK), F32),
        ],
        compiler_params=pltpu.CompilerParams(vmem_limit_bytes=12 << 20),
        name="solve",
    )(place, owner_of, gram_mine, gram_other, cross)


def send_kernel(table_ref, tiles_ref, out_ref):
    for there in range(4):
        for s in range(SLOTS):
            out_ref[there, s] = tiles_ref[table_ref[SEND + there * SLOTS + s]]


def keep_kernel(table_ref, tiles_ref, y_hbm, out_ref, y_ref, sems):
    copies = [
        pltpu.make_async_copy(y_hbm.at[table_ref[EXPERT + s]], y_ref.at[s], sems.at[s])
        for s in range(SLOTS)
    ]
    for copy in copies:
        copy.start()
    for s in range(SLOTS):
        tile = tiles_ref[table_ref[FROM + s], s]
        for z in range(4):
            out_ref[z, s] = tile
    for copy in copies:
        copy.wait()


def send(table, tiles):
    return pl.pallas_call(
        send_kernel,
        in_specs=[SM, VM],
        out_specs=VM,
        out_shape=jax.ShapeDtypeStruct((4, SLOTS) + tiles.shape[-2:], BF16),
        compiler_params=pltpu.CompilerParams(vmem_limit_bytes=8 << 20),
        name="send",
    )(table, tiles)


def keep(table, tiles, y_all):
    return pl.pallas_call(
        keep_kernel,
        in_specs=[SM, VM, HBM],
        out_specs=[VM, VM],
        out_shape=[
            jax.ShapeDtypeStruct((4, SLOTS) + tiles.shape[-2:], BF16),
            jax.ShapeDtypeStruct((SLOTS,) + y_all.shape[1:], BF16),
        ],
        scratch_shapes=[pltpu.SemaphoreType.DMA((SLOTS,))],
        compiler_params=pltpu.CompilerParams(vmem_limit_bytes=8 << 20),
        name="keep",
    )(table, tiles, pltpu.with_memory_space_constraint(y_all, pltpu.HBM))


def chip_sum(mine, other):
    return mine + lax.ppermute(other, "c", SWAP).astype(F32)


def all_sum(mine, other):
    chip = chip_sum(mine, other).astype(BF16)
    pieces = lax.all_to_all(chip, "z", 0, 0, tiled=True)
    step = (jnp.sum(pieces.astype(F32), axis=0) / D).astype(BF16)
    step_mine = lax.all_gather(step, "z", axis=0)
    return step_mine, lax.ppermute(step_mine, "c", SWAP)


def final_kernel(
    table_ref, place_ref, y_ref, mine_ref, other_ref, serving_ref, out_hbm, rows_ref, out_sems
):
    c = place_ref[0]
    slots, rows = rows_ref.shape[:2]
    count = rows // TILE

    def span(i):
        return i // count, pl.ds(pl.multiple_of(lax.rem(i, count) * TILE, TILE), TILE)

    def store(i):
        s, here = span(i)
        return pltpu.make_async_copy(rows_ref.at[s, here], out_hbm.at[s, here], out_sems.at[i])

    def step(i, carry):
        s, here = span(i)
        owned = table_ref[PRESENT + s] > 0
        y = y_ref[s, here, :]
        for half, solved in ((c, mine_ref), (1 - c, other_ref)):
            for j in range(4):
                update = jnp.dot(y, solved[j, s], preferred_element_type=F32)
                served = serving_ref[s, here, columns(half, j)].astype(F32)
                summed = served + jnp.where(owned, update, 0.0)
                rows_ref[s, here, columns(half, j)] = summed.astype(BF16)
        store(i).start()
        return carry

    lax.fori_loop(0, slots * count, step, 0)
    for i in range(slots * count):
        store(i).wait()


def final(table, place, y, mine, other, serving):
    slots, rows, _ = serving.shape
    count = slots * (rows // TILE)
    return pl.pallas_call(
        final_kernel,
        in_specs=[SM, SM, VM, VM, VM, VM],
        out_specs=HBM,
        out_shape=jax.ShapeDtypeStruct(serving.shape, BF16),
        scratch_shapes=[
            pltpu.VMEM(serving.shape, BF16),
            pltpu.SemaphoreType.DMA((count,)),
        ],
        compiler_params=pltpu.CompilerParams(vmem_limit_bytes=16 << 20),
        name="final",
    )(table, place, y, mine, other, pltpu.with_memory_space_constraint(serving, pltpu.VMEM))


def local(deltas, sketch_matrix, owner_of, serving):
    c = lax.axis_index("c").astype(jnp.int32).reshape(1)
    place = jnp.stack([lax.axis_index(a) for a in ("c", "x", "y")]).astype(jnp.int32)
    delta_rows = deltas[0]
    rows = delta_rows.shape[0]
    mine, other = first_pass(c, delta_rows, sketch_matrix)
    for iteration in range(POWER - 1):
        steps = all_sum(mine, other)
        mine, other = power_pass(power_kernel, c, delta_rows, steps, [], [], "power")
    steps = all_sum(mine, other)
    sketch, mine, other, gram_mine, gram_other = power_pass(
        last_kernel,
        c,
        delta_rows,
        steps,
        [jax.ShapeDtypeStruct((rows, RANK), BF16)],
        [jax.ShapeDtypeStruct((HALF, RANK), F32)] * 2,
        "last",
    )
    y_all = lax.all_gather(sketch, EP, axis=0)

    gram_chip = chip_sum(gram_mine, gram_other)
    gram_hi = lax.reduce_precision(gram_chip, 8, 7)
    gram_lo = (gram_chip - gram_hi).astype(BF16)
    gram_pair = jnp.concatenate([gram_hi.astype(BF16), gram_lo], axis=0)
    cross_chip = chip_sum(mine, other).astype(BF16)
    packed = jnp.concatenate(
        [cross_chip, jnp.broadcast_to(gram_pair[None], (4, RANK, RANK))], axis=1
    )
    pieces = lax.all_to_all(packed, "z", 0, 0, tiled=True)
    sums = jnp.sum(pieces.astype(F32), axis=0)
    cross = sums[:RANK]
    gram_half = sums[RANK : RANK + HALF] + sums[RANK + HALF :]
    tiles, table = solve(
        place, owner_of, gram_half, lax.ppermute(gram_half, "c", SWAP), cross
    )
    tiles = lax.all_to_all(tiles, "x", 0, 0, tiled=True)
    tiles = lax.all_to_all(send(table, tiles), "y", 0, 0, tiled=True)
    tiles, y = keep(table, tiles, y_all)
    mine = lax.all_to_all(tiles, "z", 0, 0, tiled=True)
    other = lax.ppermute(mine, "c", SWAP)
    return final(table, place, y, mine, other, serving)


def solution(mesh):
    split = Mesh(mesh.devices.reshape(4, 2, 4, 4), ("z", "c", "x", "y"))
    rows = P(EP, ("z", "c"), None)
    return jax.shard_map(
        local,
        mesh=split,
        in_specs=(rows, P(), P(), rows),
        out_specs=rows,
        check_vma=False,
    )
```

```python
import functools

import jax
import jax.numpy as jnp
from jax import lax
from jax.experimental import pallas as pl
from jax.experimental.pallas import tpu as pltpu
from jax.sharding import Mesh, PartitionSpec as P


D = 7168
FF = 2048
RANK = 256
POWER = 2
SLOTS = 2
N_EP = 16
HALF = RANK // 2
GROUP = 16
EXTRA = 16
CHUNK = FF // 8
SPANS = ((0, 256), (256, 256), (512, 384))
EP = ("x", "y")
SEND, FROM, EXPERT, PRESENT = 0, 8, 10, 12
TILE = 448
STEPS = (0, 3, 1, 2)
SWAP = [(0, 1), (1, 0)]
NT = (((1,), (1,)), ((), ()))
F32 = jnp.float32
BF16 = jnp.bfloat16
VM = pl.BlockSpec(memory_space=pltpu.VMEM)
SM = pl.BlockSpec(memory_space=pltpu.SMEM)
HBM = pl.BlockSpec(memory_space=pltpu.HBM)
TILES = (4, RANK, CHUNK)


def columns(half, j):
    return pl.ds(pl.multiple_of(half * (FF // 2) + j * CHUNK, CHUNK), CHUNK)


def load_rows(a_hbm, a_ref, sems):
    copies = [
        pltpu.make_async_copy(a_hbm.at[pl.ds(s, n)], a_ref.at[pl.ds(s, n)], sems.at[i])
        for i, (s, n) in enumerate(SPANS)
    ]
    for copy in copies:
        copy.start()
    return copies


def power_tiles(c, a_ref, yt_ref, mine_out, other_out):
    for j in range(4):
        tile = jnp.dot(yt_ref[...], a_ref[:, columns(1 - c, j)], preferred_element_type=F32)
        other_out[j] = tile.astype(BF16)
    for j in range(4):
        mine_out[j] = jnp.dot(
            yt_ref[...], a_ref[:, columns(c, j)], preferred_element_type=F32
        )


def sketch_rows(c, a_ref, s, n, mine_ref, other_ref):
    y = None
    for half, steps in ((c, mine_ref), (1 - c, other_ref)):
        for j in range(4):
            term = lax.dot_general(
                a_ref[pl.ds(s, n), columns(half, j)], steps[j], NT, preferred_element_type=F32
            )
            y = term if y is None else y + term
    return y


def first_kernel(
    c_ref, a_hbm, sketch_hbm, mine_out, other_out, a_ref, sketch_ref, yt_ref, sems, sketch_sem
):
    c = c_ref[0]
    sketch_copy = pltpu.make_async_copy(sketch_hbm, sketch_ref, sketch_sem)
    sketch_copy.start()
    copies = load_rows(a_hbm, a_ref, sems)
    sketch_copy.wait()
    for copy, (s, n) in zip(copies, SPANS):
        copy.wait()
        y = jnp.dot(a_ref[pl.ds(s, n), :], sketch_ref[...], preferred_element_type=F32)
        yt_ref[:, pl.ds(s, n)] = y.T.astype(BF16)
    power_tiles(c, a_ref, yt_ref, mine_out, other_out)


def power_kernel(c_ref, a_ref, mine_ref, other_ref, mine_out, other_out, yt_ref):
    c = c_ref[0]
    for s, n in SPANS:
        y = sketch_rows(c, a_ref, s, n, mine_ref, other_ref)
        yt_ref[:, pl.ds(s, n)] = y.T.astype(BF16)
    power_tiles(c, a_ref, yt_ref, mine_out, other_out)


def last_kernel(
    c_ref, a_ref, mine_ref, other_ref,
    y_out, mine_out, other_out, gram_mine, gram_other, yt_ref,
):
    c = c_ref[0]
    for s, n in SPANS:
        y = sketch_rows(c, a_ref, s, n, mine_ref, other_ref)
        y_out[pl.ds(s, n), :] = y.astype(BF16)
        yt_ref[:, pl.ds(s, n)] = y.T.astype(BF16)
    gram = jnp.dot(yt_ref[...], y_out[...], preferred_element_type=F32)
    top, low = gram[:HALF, :HALF], gram[HALF:, HALF:]
    row = lax.broadcasted_iota(jnp.int32, (HALF, HALF), 0)
    col = lax.broadcasted_iota(jnp.int32, (HALF, HALF), 1)
    diagonal = jnp.sum(jnp.where(row == col, top, 0.0), axis=0, keepdims=True)
    square = jnp.where(row > col, top, low)
    gram_mine[:HALF] = jnp.where(c == 0, square, gram[:HALF, HALF:])
    gram_other[:HALF] = jnp.where(c == 0, gram[:HALF, HALF:], square)
    below = jnp.broadcast_to(diagonal, (EXTRA, HALF))
    gram_mine[HALF:] = jnp.where(c == 0, below, 0.0)
    gram_other[HALF:] = jnp.where(c == 0, 0.0, below)
    power_tiles(c, a_ref, yt_ref, mine_out, other_out)


def first_pass(c, delta_rows, sketch_matrix):
    rows = delta_rows.shape[0]
    return pl.pallas_call(
        first_kernel,
        in_specs=[SM, HBM, HBM],
        out_specs=[VM] * 2,
        out_shape=[
            jax.ShapeDtypeStruct(TILES, F32),
            jax.ShapeDtypeStruct(TILES, BF16),
        ],
        scratch_shapes=[
            pltpu.VMEM(delta_rows.shape, BF16),
            pltpu.VMEM(sketch_matrix.shape, BF16),
            pltpu.VMEM((RANK, rows), BF16),
            pltpu.SemaphoreType.DMA((len(SPANS),)),
            pltpu.SemaphoreType.DMA,
        ],
        compiler_params=pltpu.CompilerParams(vmem_limit_bytes=16 << 20),
        name="first",
    )(
        c,
        pltpu.with_memory_space_constraint(delta_rows, pltpu.HBM),
        pltpu.with_memory_space_constraint(sketch_matrix, pltpu.HBM),
    )


def power_pass(kernel, c, delta_rows, steps, before, after):
    outs = before + [
        jax.ShapeDtypeStruct(TILES, F32), jax.ShapeDtypeStruct(TILES, BF16)
    ] + after
    return pl.pallas_call(
        kernel,
        in_specs=[SM, VM, VM, VM],
        out_specs=[VM] * len(outs),
        out_shape=outs,
        scratch_shapes=[pltpu.VMEM((RANK, delta_rows.shape[0]), BF16)],
        compiler_params=pltpu.CompilerParams(vmem_limit_bytes=24 << 20),
    )(c, delta_rows, *steps)


def exact_dot(a, b):
    return jnp.dot(a, b, preferred_element_type=F32, precision=lax.Precision.HIGHEST)


def invert(a_ref):
    lane = lax.broadcasted_iota(jnp.int32, (GROUP, HALF), 1)
    sub = lax.broadcasted_iota(jnp.int32, (GROUP, HALF), 0)
    lane_all = lax.broadcasted_iota(jnp.int32, (HALF, HALF), 1)

    def spread(row):
        return jnp.broadcast_to(row, (GROUP, HALF))

    def columns_of(rows, base):
        return [jnp.broadcast_to(rows[:, base + i : base + i + 1], (GROUP, HALF)) for i in range(GROUP)]

    def total(terms):
        while len(terms) > 1:
            terms = [terms[i] + terms[i + 1] for i in range(0, len(terms), 2)]
        return terms[0]

    def pivots(base, rows):
        block = columns_of(rows, base)
        for j in range(GROUP):
            inverse = 1.0 / spread(block[j][j : j + 1])
            scaled = block[j] * inverse
            new = []
            for i in range(GROUP):
                if i == j:
                    new.append(jnp.where(sub == j, -inverse, scaled))
                else:
                    t = spread(block[i][j : j + 1])
                    new.append(jnp.where(sub == j, t * inverse, block[i] - scaled * t))
            block = new
        local = lane - base
        rows = jnp.where((local >= 0) & (local < GROUP), jnp.where(local == sub, 1.0, 0.0), -rows)
        return total([block[i] * spread(rows[i : i + 1]) for i in range(GROUP)])

    rows = a_ref[:GROUP, :]
    solved = pivots(0, rows)
    for base in range(0, HALF, GROUP):
        later = base + GROUP
        if later < HALF:
            local = lane - base
            ahead = a_ref[later : later + GROUP, :]
            across = columns_of(ahead, base)
            ahead = jnp.where((local >= 0) & (local < GROUP), 0.0, ahead)
            ahead = ahead - total([across[i] * spread(solved[i : i + 1]) for i in range(GROUP)])
            ahead_solved = pivots(later, ahead)
        here = lane_all - base
        a = jnp.where((here >= 0) & (here < GROUP), 0.0, a_ref[...])
        a_ref[...] = a - lax.dot_general(
            rows, solved, (((0,), (0,)), ((), ())),
            preferred_element_type=F32, precision=lax.Precision.HIGHEST,
        )
        a_ref[base : base + GROUP, :] = solved
        if later < HALF:
            rows, solved = ahead, ahead_solved


def slots_of(owner_ref, owner):
    zero = jnp.int32(0)
    count, expert = zero, [zero] * SLOTS
    for e in range(N_EP):
        hit = owner_ref[e] == owner
        for s in range(SLOTS):
            expert[s] = jnp.where(hit & (count == s), e, expert[s])
        count = count + jnp.where(hit, 1, 0)
    return expert, [jnp.where(count > s, 1, 0) for s in range(SLOTS)]


def write_table(place_ref, owner_ref, table_ref):
    x, y = place_ref[1], place_ref[2]
    for there in range(4):
        expert, _ = slots_of(owner_ref, x * 4 + there)
        for s in range(SLOTS):
            table_ref[SEND + there * SLOTS + s] = expert[s] // 4
    expert, present = slots_of(owner_ref, x * 4 + y)
    for s in range(SLOTS):
        table_ref[FROM + s] = lax.rem(expert[s], 4)
        table_ref[EXPERT + s] = expert[s]
        table_ref[PRESENT + s] = present[s]


def solve_kernel(
    place_ref, owner_ref, mine_ref, other_ref, cross_ref, out_ref, table_ref, a_ref, b_ref
):
    write_table(place_ref, owner_ref, table_ref)
    c = place_ref[0]
    square = jnp.where(c == 0, mine_ref[...], other_ref[...])
    across = jnp.where(c == 0, other_ref[:HALF], mine_ref[:HALF])
    diagonal = square[HALF : HALF + 1]
    square = square[:HALF]
    row = lax.broadcasted_iota(jnp.int32, (HALF, HALF), 0)
    col = lax.broadcasted_iota(jnp.int32, (HALF, HALF), 1)
    lower = jnp.where(row > col, square, 0.0)
    upper = jnp.where(row < col, square, 0.0)
    a_ref[...] = lower + lower.T + jnp.where(row == col, diagonal, 0.0)
    b_ref[...] = upper + upper.T + jnp.where(row == col, square, 0.0)
    invert(a_ref)
    first = -a_ref[...]
    step = exact_dot(first, across)
    b_ref[...] = b_ref[...] - exact_dot(across.T, step)
    invert(b_ref)
    top = cross_ref[:HALF]
    low = cross_ref[HALF:]
    low_solved = -exact_dot(b_ref[...], low - exact_dot(step.T, top))
    top_solved = exact_dot(first, top) - exact_dot(step, low_solved)
    top_solved = top_solved.astype(BF16)
    low_solved = low_solved.astype(BF16)
    for x in range(4):
        out_ref[x, :HALF] = top_solved
        out_ref[x, HALF:] = low_solved


def solve(place, owner_of, gram_mine, gram_other, cross):
    return pl.pallas_call(
        solve_kernel,
        in_specs=[SM, SM, VM, VM, VM],
        out_specs=[VM, SM],
        out_shape=[
            jax.ShapeDtypeStruct((4, RANK, cross.shape[1]), BF16),
            jax.ShapeDtypeStruct((16,), jnp.int32),
        ],
        scratch_shapes=[
            pltpu.VMEM((HALF, HALF), F32),
            pltpu.VMEM((HALF, HALF), F32),
        ],
        compiler_params=pltpu.CompilerParams(vmem_limit_bytes=12 << 20),
        name="solve",
    )(place, owner_of, gram_mine, gram_other, cross)


def send_kernel(table_ref, tiles_ref, out_ref):
    for there in range(4):
        for s in range(SLOTS):
            out_ref[there, s] = tiles_ref[table_ref[SEND + there * SLOTS + s]]


def keep_kernel(table_ref, tiles_hbm, y_hbm, out_ref, y_ref, sems):
    copies = []
    for s in range(SLOTS):
        tile = tiles_hbm.at[table_ref[FROM + s], s]
        copies.append(pltpu.make_async_copy(tile, out_ref.at[s], sems.at[s, 0]))
        sketch = y_hbm.at[table_ref[EXPERT + s]]
        copies.append(pltpu.make_async_copy(sketch, y_ref.at[s], sems.at[s, 1]))
    for copy in copies:
        copy.start()
    for copy in copies:
        copy.wait()


def send(table, tiles):
    return pl.pallas_call(
        send_kernel,
        in_specs=[SM, VM],
        out_specs=VM,
        out_shape=jax.ShapeDtypeStruct((4, SLOTS) + tiles.shape[-2:], BF16),
        compiler_params=pltpu.CompilerParams(vmem_limit_bytes=8 << 20),
        name="send",
    )(table, tiles)


def keep(table, tiles, y_all):
    return pl.pallas_call(
        keep_kernel,
        in_specs=[SM, HBM, HBM],
        out_specs=[VM, VM],
        out_shape=[
            jax.ShapeDtypeStruct(tiles.shape[1:], BF16),
            jax.ShapeDtypeStruct((SLOTS,) + y_all.shape[1:], BF16),
        ],
        scratch_shapes=[pltpu.SemaphoreType.DMA((SLOTS, 2))],
        compiler_params=pltpu.CompilerParams(vmem_limit_bytes=8 << 20),
        name="keep",
    )(
        table,
        pltpu.with_memory_space_constraint(tiles, pltpu.HBM),
        pltpu.with_memory_space_constraint(y_all, pltpu.HBM),
    )


def chip_sum(mine, other):
    return mine + lax.ppermute(other, "c", SWAP).astype(F32)


def all_sum(mine, other):
    chip = chip_sum(mine, other).astype(BF16)
    pieces = lax.all_to_all(chip, "z", 0, 0, tiled=True)
    step = (jnp.sum(pieces.astype(F32), axis=0) / D).astype(BF16)
    step_mine = lax.all_to_all(
        jnp.broadcast_to(step[None], (4,) + step.shape), "z", 0, 0, tiled=True
    )
    return step_mine, lax.ppermute(step_mine, "c", SWAP)


def final_kernel(
    step, table_ref, place_ref, y_ref, mine_ref, other_ref, serving_ref, begun_hbm, out_hbm, rows_ref, sems
):
    del begun_hbm
    c = place_ref[0]
    there = lax.rem(place_ref[3] + step, 4)
    slots, rows = rows_ref.shape[1:3]
    count = rows // TILE

    def span(i):
        return i // count, pl.ds(pl.multiple_of(lax.rem(i, count) * TILE, TILE), TILE)

    def store(i, side):
        s, here = span(i)
        half = c if side == 0 else 1 - c
        return pltpu.make_async_copy(
            rows_ref.at[side, s, here],
            out_hbm.at[s, here, columns(half, there)],
            sems.at[side, i],
        )

    def update(i, carry):
        s, here = span(i)
        owned = table_ref[PRESENT + s] > 0
        y = y_ref[s, here, :]
        for side, tiles in enumerate((mine_ref, other_ref)):
            half = c if side == 0 else 1 - c
            term = jnp.dot(y, tiles[s], preferred_element_type=F32)
            served = serving_ref[s, here, columns(half, there)].astype(F32)
            summed = served + jnp.where(owned, term, 0.0)
            rows_ref[side, s, here, :] = summed.astype(BF16)
            store(i, side).start()
        return carry

    lax.fori_loop(0, slots * count, update, 0)
    for i in range(slots * count):
        for side in range(2):
            store(i, side).wait()


def final_first_kernel(step, table_ref, place_ref, y_ref, mine_ref, other_ref, serving_ref, *refs):
    final_kernel(step, table_ref, place_ref, y_ref, mine_ref, other_ref, serving_ref, None, *refs)


def final(step, table, place, y, mine, other, serving, begun):
    slots, rows, _ = serving.shape
    more = [] if begun is None else [begun]
    kernel = final_first_kernel if begun is None else final_kernel
    return pl.pallas_call(
        functools.partial(kernel, step),
        in_specs=[SM, SM, VM, VM, VM, VM] + [HBM] * len(more),
        out_specs=HBM,
        out_shape=jax.ShapeDtypeStruct(serving.shape, BF16),
        input_output_aliases={6: 0} if more else {},
        scratch_shapes=[
            pltpu.VMEM((2, slots, rows, CHUNK), BF16),
            pltpu.SemaphoreType.DMA((2, slots * (rows // TILE))),
        ],
        compiler_params=pltpu.CompilerParams(vmem_limit_bytes=6 << 20),
        cost_estimate=pl.CostEstimate(
            flops=serving.size * RANK // 2, bytes_accessed=serving.size, transcendentals=0
        ),
        name="final",
    )(table, place, y, mine, other, serving, *more)


def local(deltas, sketch_matrix, owner_of, serving):
    c = lax.axis_index("c").astype(jnp.int32).reshape(1)
    place = jnp.stack([lax.axis_index(a) for a in ("c", "x", "y", "z")]).astype(jnp.int32)
    delta_rows = deltas[0]
    rows = delta_rows.shape[0]
    mine, other = first_pass(c, delta_rows, sketch_matrix)
    for _ in range(POWER - 1):
        steps = all_sum(mine, other)
        mine, other = power_pass(power_kernel, c, delta_rows, steps, [], [])
    steps = all_sum(mine, other)
    sketch, mine, other, gram_mine, gram_other = power_pass(
        last_kernel,
        c,
        delta_rows,
        steps,
        [jax.ShapeDtypeStruct((rows, RANK), BF16)],
        [jax.ShapeDtypeStruct((HALF + EXTRA, HALF), F32)] * 2,
    )
    y_all = lax.all_gather(sketch, EP, axis=0)

    gram_chip = chip_sum(gram_mine, gram_other)
    gram_hi = lax.reduce_precision(gram_chip, 8, 7)
    gram_lo = (gram_chip - gram_hi).astype(BF16)
    gram_pair = jnp.concatenate([gram_hi.astype(BF16), gram_lo], axis=1)
    cross_chip = chip_sum(mine, other).astype(BF16)
    packed = jnp.concatenate(
        [cross_chip, jnp.broadcast_to(gram_pair[None], (4,) + gram_pair.shape)], axis=1
    )
    pieces = lax.all_to_all(packed, "z", 0, 0, tiled=True)
    sums = jnp.sum(pieces.astype(F32), axis=0)
    cross = sums[:RANK]
    gram_half = sums[RANK:, :HALF] + sums[RANK:, HALF:]
    tiles, table = solve(
        place, owner_of, gram_half, lax.ppermute(gram_half, "c", SWAP), cross
    )
    tiles = lax.all_to_all(tiles, "x", 0, 0, tiled=True)
    tiles = lax.all_to_all(send(table, tiles), "y", 0, 0, tiled=True)
    tile, y = keep(table, tiles, y_all)
    serving = pltpu.with_memory_space_constraint(serving, pltpu.VMEM)
    moved = {0: tile}
    updated = None
    for step in STEPS[1:]:
        moved[step] = lax.ppermute(tile, "z", [((z + step) % 4, z) for z in range(4)])
    for step in STEPS:
        other = lax.ppermute(moved[step], "c", SWAP)
        updated = final(step, table, place, y, moved[step], other, serving, updated)
    return updated


def solution(mesh):
    split = Mesh(mesh.devices.reshape(4, 2, 4, 4), ("z", "c", "x", "y"))
    rows = P(EP, ("z", "c"), None)
    return jax.shard_map(
        local,
        mesh=split,
        in_specs=(rows, P(), P(), rows),
        out_specs=rows,
        check_vma=False,
    )
```

```python
import functools

import jax
import jax.numpy as jnp
from jax import lax
from jax.experimental import pallas as pl
from jax.experimental.pallas import tpu as pltpu
from jax.sharding import Mesh, PartitionSpec as P


D = 7168
FF = 2048
RANK = 256
POWER = 2
SLOTS = 2
N_EP = 16
HALF = RANK // 2
GROUP = 16
EXTRA = 16
CHUNK = FF // 8
SPANS = ((0, 256), (256, 256), (512, 384))
EP = ("x", "y")
SEND, FROM, EXPERT, PRESENT = 0, 8, 10, 12
TILE = 448
STEPS = (0, 3, 1, 2)
STAGES = (
    ((0, False), (0, True)),
    ((3, False),),
    ((3, True),),
    ((1, False),),
    ((1, True), (2, False)),
    ((2, True),),
)
SWAP = [(0, 1), (1, 0)]
NT = (((1,), (1,)), ((), ()))
F32 = jnp.float32
BF16 = jnp.bfloat16
VM = pl.BlockSpec(memory_space=pltpu.VMEM)
SM = pl.BlockSpec(memory_space=pltpu.SMEM)
HBM = pl.BlockSpec(memory_space=pltpu.HBM)
TILES = (4, RANK, CHUNK)


def columns(half, j):
    return pl.ds(pl.multiple_of(half * (FF // 2) + j * CHUNK, CHUNK), CHUNK)


def load_rows(a_hbm, a_ref, sems):
    copies = [
        pltpu.make_async_copy(a_hbm.at[pl.ds(s, n)], a_ref.at[pl.ds(s, n)], sems.at[i])
        for i, (s, n) in enumerate(SPANS)
    ]
    for copy in copies:
        copy.start()
    return copies


def power_tiles(c, a_ref, yt_ref, mine_out, other_out):
    for j in range(4):
        tile = jnp.dot(yt_ref[...], a_ref[:, columns(1 - c, j)], preferred_element_type=F32)
        other_out[j] = tile.astype(BF16)
    for j in range(4):
        mine_out[j] = jnp.dot(
            yt_ref[...], a_ref[:, columns(c, j)], preferred_element_type=F32
        )


def sketch_rows(c, a_ref, s, n, mine_ref, other_ref):
    y = None
    for half, steps in ((c, mine_ref), (1 - c, other_ref)):
        for j in range(4):
            term = lax.dot_general(
                a_ref[pl.ds(s, n), columns(half, j)], steps[j], NT, preferred_element_type=F32
            )
            y = term if y is None else y + term
    return y


def first_kernel(
    a_hbm, sketch_hbm, mine_out, other_out, a_ref, sketch_ref, yt_ref, sems, sketch_sem
):
    c = lax.axis_index("c")
    sketch_copy = pltpu.make_async_copy(sketch_hbm, sketch_ref, sketch_sem)
    sketch_copy.start()
    copies = load_rows(a_hbm, a_ref, sems)
    sketch_copy.wait()
    for copy, (s, n) in zip(copies, SPANS):
        copy.wait()
        y = jnp.dot(a_ref[pl.ds(s, n), :], sketch_ref[...], preferred_element_type=F32)
        yt_ref[:, pl.ds(s, n)] = y.T.astype(BF16)
    power_tiles(c, a_ref, yt_ref, mine_out, other_out)


def power_kernel(a_ref, mine_ref, other_ref, mine_out, other_out, yt_ref):
    c = lax.axis_index("c")
    for s, n in SPANS:
        y = sketch_rows(c, a_ref, s, n, mine_ref, other_ref)
        yt_ref[:, pl.ds(s, n)] = y.T.astype(BF16)
    power_tiles(c, a_ref, yt_ref, mine_out, other_out)


def last_kernel(
    a_ref, mine_ref, other_ref,
    y_out, mine_out, other_out, gram_mine, gram_other, yt_ref,
):
    c = lax.axis_index("c")
    for s, n in SPANS:
        y = sketch_rows(c, a_ref, s, n, mine_ref, other_ref)
        y_out[pl.ds(s, n), :] = y.astype(BF16)
        yt_ref[:, pl.ds(s, n)] = y.T.astype(BF16)
    gram = jnp.dot(yt_ref[...], y_out[...], preferred_element_type=F32)
    top, low = gram[:HALF, :HALF], gram[HALF:, HALF:]
    row = lax.broadcasted_iota(jnp.int32, (HALF, HALF), 0)
    col = lax.broadcasted_iota(jnp.int32, (HALF, HALF), 1)
    diagonal = jnp.sum(jnp.where(row == col, top, 0.0), axis=0, keepdims=True)
    square = jnp.where(row > col, top, low)
    gram_mine[:HALF] = jnp.where(c == 0, square, gram[:HALF, HALF:])
    gram_other[:HALF] = jnp.where(c == 0, gram[:HALF, HALF:], square)
    below = jnp.broadcast_to(diagonal, (EXTRA, HALF))
    gram_mine[HALF:] = jnp.where(c == 0, below, 0.0)
    gram_other[HALF:] = jnp.where(c == 0, 0.0, below)
    power_tiles(c, a_ref, yt_ref, mine_out, other_out)


def first_pass(delta_rows, sketch_matrix):
    rows = delta_rows.shape[0]
    return pl.pallas_call(
        first_kernel,
        in_specs=[HBM, HBM],
        out_specs=[VM] * 2,
        out_shape=[
            jax.ShapeDtypeStruct(TILES, F32),
            jax.ShapeDtypeStruct(TILES, BF16),
        ],
        scratch_shapes=[
            pltpu.VMEM(delta_rows.shape, BF16),
            pltpu.VMEM(sketch_matrix.shape, BF16),
            pltpu.VMEM((RANK, rows), BF16),
            pltpu.SemaphoreType.DMA((len(SPANS),)),
            pltpu.SemaphoreType.DMA,
        ],
        compiler_params=pltpu.CompilerParams(vmem_limit_bytes=16 << 20),
        name="first",
    )(
        pltpu.with_memory_space_constraint(delta_rows, pltpu.HBM),
        pltpu.with_memory_space_constraint(sketch_matrix, pltpu.HBM),
    )


def power_pass(kernel, delta_rows, steps, before, after):
    outs = before + [
        jax.ShapeDtypeStruct(TILES, F32), jax.ShapeDtypeStruct(TILES, BF16)
    ] + after
    return pl.pallas_call(
        kernel,
        in_specs=[VM, VM, VM],
        out_specs=[VM] * len(outs),
        out_shape=outs,
        scratch_shapes=[pltpu.VMEM((RANK, delta_rows.shape[0]), BF16)],
        compiler_params=pltpu.CompilerParams(vmem_limit_bytes=24 << 20),
    )(delta_rows, *steps)


def exact_dot(a, b):
    return jnp.dot(a, b, preferred_element_type=F32, precision=lax.Precision.HIGHEST)


def invert(a_ref):
    lane = lax.broadcasted_iota(jnp.int32, (GROUP, HALF), 1)
    sub = lax.broadcasted_iota(jnp.int32, (GROUP, HALF), 0)
    lane_all = lax.broadcasted_iota(jnp.int32, (HALF, HALF), 1)

    def spread(row):
        return jnp.broadcast_to(row, (GROUP, HALF))

    def columns_of(rows, base):
        return [jnp.broadcast_to(rows[:, base + i : base + i + 1], (GROUP, HALF)) for i in range(GROUP)]

    def total(terms):
        while len(terms) > 1:
            terms = [terms[i] + terms[i + 1] for i in range(0, len(terms), 2)]
        return terms[0]

    def pivots(base, rows):
        block = columns_of(rows, base)
        for j in range(GROUP):
            inverse = 1.0 / spread(block[j][j : j + 1])
            scaled = block[j] * inverse
            new = []
            for i in range(GROUP):
                if i == j:
                    new.append(jnp.where(sub == j, -inverse, scaled))
                else:
                    t = spread(block[i][j : j + 1])
                    new.append(jnp.where(sub == j, t * inverse, block[i] - scaled * t))
            block = new
        local = lane - base
        rows = jnp.where((local >= 0) & (local < GROUP), jnp.where(local == sub, 1.0, 0.0), -rows)
        return total([block[i] * spread(rows[i : i + 1]) for i in range(GROUP)])

    rows = a_ref[:GROUP, :]
    solved = pivots(0, rows)
    for base in range(0, HALF, GROUP):
        later = base + GROUP
        if later < HALF:
            local = lane - base
            ahead = a_ref[later : later + GROUP, :]
            across = columns_of(ahead, base)
            ahead = jnp.where((local >= 0) & (local < GROUP), 0.0, ahead)
            ahead = ahead - total([across[i] * spread(solved[i : i + 1]) for i in range(GROUP)])
            ahead_solved = pivots(later, ahead)
        here = lane_all - base
        a = jnp.where((here >= 0) & (here < GROUP), 0.0, a_ref[...])
        a_ref[...] = a - lax.dot_general(
            rows, solved, (((0,), (0,)), ((), ())),
            preferred_element_type=F32, precision=lax.Precision.HIGHEST,
        )
        a_ref[base : base + GROUP, :] = solved
        if later < HALF:
            rows, solved = ahead, ahead_solved


def slots_of(owner_ref, owner):
    zero = jnp.int32(0)
    count, expert = zero, [zero] * SLOTS
    for e in range(N_EP):
        hit = owner_ref[e] == owner
        for s in range(SLOTS):
            expert[s] = jnp.where(hit & (count == s), e, expert[s])
        count = count + jnp.where(hit, 1, 0)
    return expert, [jnp.where(count > s, 1, 0) for s in range(SLOTS)]


def write_table(owner_ref, table_ref):
    x, y = lax.axis_index("x"), lax.axis_index("y")
    for there in range(4):
        expert, _ = slots_of(owner_ref, x * 4 + there)
        for s in range(SLOTS):
            table_ref[SEND + there * SLOTS + s] = expert[s] // 4
    expert, present = slots_of(owner_ref, x * 4 + y)
    for s in range(SLOTS):
        table_ref[FROM + s] = lax.rem(expert[s], 4)
        table_ref[EXPERT + s] = expert[s]
        table_ref[PRESENT + s] = present[s]


def solve_kernel(
    owner_ref, mine_ref, other_ref, cross_ref, out_ref, table_ref, a_ref, b_ref
):
    write_table(owner_ref, table_ref)
    c = lax.axis_index("c")
    square = jnp.where(c == 0, mine_ref[...], other_ref[...])
    across = jnp.where(c == 0, other_ref[:HALF], mine_ref[:HALF])
    diagonal = square[HALF : HALF + 1]
    square = square[:HALF]
    row = lax.broadcasted_iota(jnp.int32, (HALF, HALF), 0)
    col = lax.broadcasted_iota(jnp.int32, (HALF, HALF), 1)
    lower = jnp.where(row > col, square, 0.0)
    upper = jnp.where(row < col, square, 0.0)
    a_ref[...] = lower + lower.T + jnp.where(row == col, diagonal, 0.0)
    b_ref[...] = upper + upper.T + jnp.where(row == col, square, 0.0)
    invert(a_ref)
    first = -a_ref[...]
    step = exact_dot(first, across)
    b_ref[...] = b_ref[...] - exact_dot(across.T, step)
    invert(b_ref)
    top = cross_ref[:HALF]
    low = cross_ref[HALF:]
    low_solved = -exact_dot(b_ref[...], low - exact_dot(step.T, top))
    top_solved = exact_dot(first, top) - exact_dot(step, low_solved)
    top_solved = top_solved.astype(BF16)
    low_solved = low_solved.astype(BF16)
    out_ref[:HALF] = top_solved
    out_ref[HALF:] = low_solved


def solve(owner_of, gram_mine, gram_other, cross):
    return pl.pallas_call(
        solve_kernel,
        in_specs=[SM, VM, VM, VM],
        out_specs=[VM, SM],
        out_shape=[
            jax.ShapeDtypeStruct((RANK, cross.shape[1]), BF16),
            jax.ShapeDtypeStruct((16,), jnp.int32),
        ],
        scratch_shapes=[
            pltpu.VMEM((HALF, HALF), F32),
            pltpu.VMEM((HALF, HALF), F32),
        ],
        compiler_params=pltpu.CompilerParams(vmem_limit_bytes=12 << 20),
        name="solve",
    )(owner_of, gram_mine, gram_other, cross)


def send_kernel(table_ref, *refs):
    tiles_refs, out_refs, all_ref = refs[:4], refs[4:8], refs[8]
    for step, tile_ref in enumerate(tiles_refs):
        all_ref[lax.rem(lax.axis_index("x") - step + 4, 4)] = tile_ref[...]
    for step, out_ref in enumerate(out_refs):
        there = lax.rem(lax.axis_index("y") + step, 4)
        for s in range(SLOTS):
            out_ref[s] = all_ref[table_ref[SEND + there * SLOTS + s]]


def keep_kernel(table_ref, *refs):
    *tiles_hbm, y_hbm, out_ref, y_ref, sems = refs

    def tile_copy(s, tiles):
        return pltpu.make_async_copy(tiles.at[s], out_ref.at[s], sems.at[s, 0])

    def sketch_copy(s):
        sketch = y_hbm.at[table_ref[EXPERT + s]]
        return pltpu.make_async_copy(sketch, y_ref.at[s], sems.at[s, 1])

    for s in range(SLOTS):
        present = table_ref[PRESENT + s] > 0
        steps = lax.rem(lax.axis_index("y") - table_ref[FROM + s] + 4, 4)

        @pl.when(present)
        def _():
            sketch_copy(s).start()

        for step, tiles in enumerate(tiles_hbm):

            @pl.when(present & (steps == step))
            def _():
                tile_copy(s, tiles).start()

        @pl.when(table_ref[PRESENT + s] == 0)
        def _():
            out_ref[s] = jnp.zeros_like(out_ref[s])
            y_ref[s] = jnp.zeros_like(y_ref[s])

    for s in range(SLOTS):

        @pl.when(table_ref[PRESENT + s] > 0)
        def _():
            tile_copy(s, tiles_hbm[0]).wait()
            sketch_copy(s).wait()


def send(table, tiles):
    shape = tiles[0].shape
    return pl.pallas_call(
        send_kernel,
        in_specs=[SM] + [VM] * 4,
        out_specs=[VM] * 4,
        out_shape=[jax.ShapeDtypeStruct((SLOTS,) + shape, BF16)] * 4,
        scratch_shapes=[pltpu.VMEM((4,) + shape, BF16)],
        compiler_params=pltpu.CompilerParams(vmem_limit_bytes=8 << 20),
        name="send",
    )(table, *tiles)


def keep(table, tiles, y_all):
    return pl.pallas_call(
        keep_kernel,
        in_specs=[SM] + [HBM] * 5,
        out_specs=[VM, VM],
        out_shape=[
            jax.ShapeDtypeStruct(tiles[0].shape, BF16),
            jax.ShapeDtypeStruct((SLOTS,) + y_all.shape[1:], BF16),
        ],
        scratch_shapes=[pltpu.SemaphoreType.DMA((SLOTS, 2))],
        compiler_params=pltpu.CompilerParams(vmem_limit_bytes=8 << 20),
        name="keep",
    )(
        table,
        *(pltpu.with_memory_space_constraint(t, pltpu.HBM) for t in tiles),
        pltpu.with_memory_space_constraint(y_all, pltpu.HBM),
    )


def chip_sum(mine, other):
    return mine + lax.ppermute(other, "c", SWAP).astype(F32)


def all_sum(mine, other):
    chip = chip_sum(mine, other).astype(BF16)
    pieces = lax.all_to_all(chip, "z", 0, 0, tiled=True)
    step = (jnp.sum(pieces.astype(F32), axis=0) / D).astype(BF16)
    step_mine = lax.all_to_all(
        jnp.broadcast_to(step[None], (4,) + step.shape), "z", 0, 0, tiled=True
    )
    return step_mine, lax.ppermute(step_mine, "c", SWAP)


def final_kernel(parts, y_ref, serving_ref, *refs):
    tiles_refs, (out_hbm, rows_ref, sems) = refs[: len(parts)], refs[-3:]
    c = lax.axis_index("c")
    slots, rows = rows_ref.shape[1:3]
    count = rows // TILE

    def span(i):
        return i // count, pl.ds(pl.multiple_of(lax.rem(i, count) * TILE, TILE), TILE)

    def side(p):
        step, shared = parts[p]
        there = lax.rem(lax.axis_index("z") + step, 4)
        return columns(1 - c if shared else c, there)

    def store(i, p):
        s, here = span(i)
        return pltpu.make_async_copy(
            rows_ref.at[p, s, here], out_hbm.at[s, here, side(p)], sems.at[p, i]
        )

    def update(i, carry):
        s, here = span(i)
        y = y_ref[s, here, :]
        for p, tiles in enumerate(tiles_refs):
            term = jnp.dot(y, tiles[s], preferred_element_type=F32)
            served = serving_ref[s, here, side(p)].astype(F32)
            rows_ref[p, s, here, :] = (served + term).astype(BF16)
            store(i, p).start()
        return carry

    lax.fori_loop(0, slots * count, update, 0)
    for i in range(slots * count):
        for p in range(len(parts)):
            store(i, p).wait()


def final(parts, tiles, y, serving, begun):
    slots, rows, _ = serving.shape
    more = [] if begun is None else [begun]
    return pl.pallas_call(
        functools.partial(final_kernel, parts),
        in_specs=[VM, VM] + [VM] * len(parts) + [HBM] * len(more),
        out_specs=HBM,
        out_shape=jax.ShapeDtypeStruct(serving.shape, BF16),
        input_output_aliases={2 + len(parts): 0} if more else {},
        scratch_shapes=[
            pltpu.VMEM((len(parts), slots, rows, CHUNK), BF16),
            pltpu.SemaphoreType.DMA((len(parts), slots * (rows // TILE))),
        ],
        compiler_params=pltpu.CompilerParams(vmem_limit_bytes=6 << 20),
        cost_estimate=pl.CostEstimate(
            flops=serving.size * RANK // 4 * len(parts),
            bytes_accessed=serving.size // 2 * len(parts),
            transcendentals=0,
        ),
        name="final",
    )(y, serving, *tiles, *more)


def local(deltas, sketch_matrix, owner_of, serving):
    delta_rows = deltas[0]
    rows = delta_rows.shape[0]
    mine, other = first_pass(delta_rows, sketch_matrix)
    for _ in range(POWER - 1):
        steps = all_sum(mine, other)
        mine, other = power_pass(power_kernel, delta_rows, steps, [], [])
    steps = all_sum(mine, other)
    sketch, mine, other, gram_mine, gram_other = power_pass(
        last_kernel,
        delta_rows,
        steps,
        [jax.ShapeDtypeStruct((rows, RANK), BF16)],
        [jax.ShapeDtypeStruct((HALF + EXTRA, HALF), F32)] * 2,
    )
    y_all = lax.all_gather(sketch, EP, axis=0)

    gram_chip = chip_sum(gram_mine, gram_other)
    gram_hi = lax.reduce_precision(gram_chip, 8, 7)
    gram_lo = (gram_chip - gram_hi).astype(BF16)
    gram_pair = jnp.concatenate([gram_hi.astype(BF16), gram_lo], axis=1)
    cross_chip = chip_sum(mine, other).astype(BF16)
    packed = jnp.concatenate(
        [cross_chip, jnp.broadcast_to(gram_pair[None], (4,) + gram_pair.shape)], axis=1
    )
    pieces = lax.all_to_all(packed, "z", 0, 0, tiled=True)
    sums = jnp.sum(pieces.astype(F32), axis=0)
    cross = sums[:RANK]
    gram_half = sums[RANK:, :HALF] + sums[RANK:, HALF:]
    solved, table = solve(
        owner_of, gram_half, lax.ppermute(gram_half, "c", SWAP), cross
    )
    tiles = [solved] + [
        lax.ppermute(solved, "x", [(x, (x + step) % 4) for x in range(4)]) for step in range(1, 4)
    ]
    tiles = list(send(table, tiles))
    for step in range(1, 4):
        tiles[step] = lax.ppermute(tiles[step], "y", [(y, (y + step) % 4) for y in range(4)])
    tile, y = keep(table, tiles, y_all)
    serving = pltpu.with_memory_space_constraint(serving, pltpu.VMEM)
    held = {(0, False): tile}
    updated = None
    for step in STEPS[1:]:
        held[step, False] = lax.ppermute(
            tile, "z", [((z + step) % 4, z) for z in range(4)]
        )
    for step in STEPS:
        held[step, True] = lax.ppermute(held[step, False], "c", SWAP)
    for parts in STAGES:
        updated = final(parts, [held[part] for part in parts], y, serving, updated)
    return updated


def solution(mesh):
    split = Mesh(mesh.devices.reshape(4, 2, 4, 4), ("z", "c", "x", "y"))
    rows = P(EP, ("z", "c"), None)
    return jax.shard_map(
        local,
        mesh=split,
        in_specs=(rows, P(), P(), rows),
        out_specs=rows,
        check_vma=False,
    )
```
